32 devices in a mesh: rep: 4 (over y, x), exp: 8 (over z, core).
Axes of the slice: x: 2, y: 2, z: 4, core: 2. Of those that a mesh axis runs over, the one named last changes fastest.
Arguments:
- tokens: bfloat16 [4096, 3584], P(('rep', 'exp')), may hold values from -6 to 6
- routes: int32 [4096, 8], P(('rep', 'exp')), may hold values from 0 to 255, as said below
- gates: float32 [4096, 8], P(('rep', 'exp')), may hold values from 0.1 to 1
- gate_weight: bfloat16 [8, 3584, 2048], P('exp', None, 'rep'), may hold values from -0.09375 to 0.09375
- up_weight: bfloat16 [8, 3584, 2048], P('exp', None, 'rep'), may hold values from -0.09375 to 0.09375
- down_weight: bfloat16 [8, 2048, 3584], P('exp', 'rep'), may hold values from -0.125 to 0.125
- grad_out: bfloat16 [4096, 3584], P(('rep', 'exp')), may hold values from -6 to 6
Outputs:
- combined: bfloat16 [4096, 3584], P(('rep', 'exp'))
- token_grad: bfloat16 [4096, 3584], P(('rep', 'exp'))
- gate_weight_grad: bfloat16 [8, 3584, 2048], P('exp', None, 'rep')
- up_weight_grad: bfloat16 [8, 3584, 2048], P('exp', None, 'rep')
- down_weight_grad: bfloat16 [8, 2048, 3584], P('exp', 'rep')
The draws below stay inside these ranges and needn't reach their ends.
Inputs may be any that keep to these rules, and one draw needn't show every extreme that they name: `routes`: each row names 8 different experts and at most one of experts 0 to 7. In the rows of one device (aligned blocks of 128 rows) each of experts 0 to 7 is named by at most 2 rows, and one of them, the same in every block, by exactly 2 rows.
All inputs are finite; a program needn't handle non-finite values.
Results may differ from the reference program's by a relative error of at most 0.012.
Values may be sent and summed in bfloat16 or wider, within the bound.
A program may use at most 128 MiB of HBM per device.

```python
import jax
import jax.numpy as jnp
from jax import lax

D = 3584
FF = 2048
EXPERTS = 256
TOP = 8
CAP = 2
TOK_DEV = 128
TOKENS = 4096
N_REP = 4
N_EXP = 8


def draw_routes(key, part):
    blocks = N_REP * N_EXP
    live_count = N_EXP
    spare_ids = EXPERTS - live_count
    stride = spare_ids // TOP
    slot_total = live_count * CAP
    key_hot, key_counts, key_perm, key_column, key_first = jax.random.split(key, 5)
    hottest = jax.random.randint(key_hot, (), 0, live_count)
    counts = jax.random.randint(key_counts, (blocks, live_count), 0, CAP + 1)
    counts = jnp.where(jnp.arange(live_count)[None, :] == hottest, CAP, counts)
    orders = jax.vmap(lambda sub_key: jax.random.permutation(sub_key, TOK_DEV))(jax.random.split(key_perm, blocks))
    slot_ids = jnp.arange(slot_total)
    slot_expert = slot_ids // CAP
    slot_rank = slot_ids % CAP
    is_live = slot_rank[None, :] < counts[:, slot_expert]
    targets = orders[:, :slot_total]
    inside = jnp.full((blocks, TOK_DEV), -1, jnp.int32)
    inside = inside.at[jnp.arange(blocks)[:, None], targets].set(jnp.where(is_live, slot_expert[None, :], -1).astype(jnp.int32))
    inside = inside.reshape(blocks * TOK_DEV)
    column = jax.random.randint(key_column, (blocks * TOK_DEV,), 0, TOP)
    first_id = jax.random.randint(key_first, (blocks * TOK_DEV,), 0, spare_ids)
    outside = live_count + (first_id[:, None] + jnp.arange(TOP)[None, :] * stride) % spare_ids
    chosen = (jnp.arange(TOP)[None, :] == column[:, None]) & (inside[:, None] >= 0)
    return jnp.where(chosen, inside[:, None], outside).astype(jnp.int32)


def levels(stream_key, extent, shards, least, high):
    gain, own = 1.0, jax.random.fold_in(stream_key, 6)
    for dim, parts in shards:
        draws = jnp.exp(jax.random.uniform(jax.random.fold_in(own, dim), (parts,), jnp.float32, least / len(shards), high / len(shards)))
        gain = gain * jnp.repeat(draws, extent[dim] // parts).reshape([-1 if axis == dim else 1 for axis in range(len(extent))])
    return gain


def normal_values(rng, extent, spread, most, cuts=(), held_as=jnp.bfloat16):
    values = spread * jax.random.normal(rng, extent, jnp.float32)
    if cuts:
        values = values * levels(rng, extent, cuts, -0.22, 0.18)
    return jnp.clip(values, -most, most).astype(held_as)


def setup_inputs(seed: int = 0) -> dict:
    keys = jax.random.split(jax.random.key(seed), 8)
    return {
        "tokens": normal_values(keys[0], (TOKENS, D), 1.0, 6.0, ((0, 32),)),
        "routes": draw_routes(jax.random.fold_in(keys[7], 71), 0),
        "gates": jnp.clip(0.1 + 0.9 * jax.random.uniform(keys[2], (TOKENS, TOP), jnp.float32) ** levels(keys[2], (TOKENS, TOP), ((0, 32),), -0.2, 0.2), 0.1, 1.0),
        "gate_weight": normal_values(keys[3], (N_EXP, D, FF), D ** -0.5, 0.09375, ((0, 8), (2, 4))),
        "up_weight": normal_values(keys[4], (N_EXP, D, FF), D ** -0.5, 0.09375, ((0, 8), (2, 4))),
        "down_weight": normal_values(keys[5], (N_EXP, FF, D), FF ** -0.5, 0.125, ((0, 8), (1, 4))),
        "grad_out": normal_values(keys[6], (TOKENS, D), 1.0, 6.0, ((0, 32),)),
    }


def block_sum(left, right, pattern):
    rounded = lax.optimization_barrier(jnp.einsum(pattern, left, right).astype(jnp.bfloat16))
    return jnp.sum(rounded.astype(jnp.float32), axis=1)


def reference(tokens, routes, gates, gate_weight, up_weight, down_weight, grad_out):
    capacity = N_REP * N_EXP * CAP
    blocks = N_REP
    block_units = FF // blocks
    live_count = N_EXP
    total_tokens = tokens.shape[0]
    features = tokens.shape[1]
    token_ids = jnp.arange(total_tokens, dtype=jnp.int32)

    def per_expert(carry, inputs):
        out_total, grad_total = carry
        expert, w_gate, w_up, w_down = inputs
        matches = routes == expert
        picked = jnp.any(matches, axis=1)
        weight = jnp.sum(jnp.where(matches, gates, jnp.zeros((), gates.dtype)), axis=1)
        order = (jnp.cumsum(picked.astype(jnp.int32)) - 1).astype(jnp.int32)
        target = jnp.where(picked, order, capacity).astype(jnp.int32)
        source = jnp.zeros((capacity + 1,), jnp.int32).at[target].set(token_ids)[:capacity]
        filled = jnp.zeros((capacity + 1,), gates.dtype).at[target].set(1.0)[:capacity]
        row_gate = weight[source] * filled
        rows_in = jnp.where(filled[:, None] > 0, tokens[source], jnp.zeros((), tokens.dtype))
        gate_pre = jnp.dot(rows_in, w_gate, preferred_element_type=jnp.float32)
        up_pre = jnp.dot(rows_in, w_up, preferred_element_type=jnp.float32)
        sigmoid_gate = jax.nn.sigmoid(gate_pre)
        active = gate_pre * sigmoid_gate
        hidden = (active * up_pre).astype(jnp.bfloat16)
        expert_out = block_sum(
            hidden.astype(jnp.float32).reshape(capacity, blocks, block_units),
            w_down.astype(jnp.float32).reshape(blocks, block_units, features),
            "rbf,bfd->rbd").astype(jnp.bfloat16)
        out_total = out_total.at[source].add(row_gate[:, None] * expert_out.astype(jnp.float32))
        out_grad = (row_gate[:, None] * grad_out[source].astype(jnp.float32)).astype(jnp.bfloat16)
        hidden_grad = jnp.dot(out_grad, w_down.T, preferred_element_type=jnp.float32)
        gate_grad = (hidden_grad * up_pre * sigmoid_gate * (1.0 + gate_pre * (1.0 - sigmoid_gate))).astype(jnp.bfloat16)
        up_grad = (hidden_grad * active).astype(jnp.bfloat16)
        down_grad = jnp.dot(hidden.T, out_grad, preferred_element_type=jnp.float32).astype(jnp.bfloat16)
        gate_wgrad = jnp.dot(rows_in.T, gate_grad, preferred_element_type=jnp.float32).astype(jnp.bfloat16)
        up_wgrad = jnp.dot(rows_in.T, up_grad, preferred_element_type=jnp.float32).astype(jnp.bfloat16)
        both_grad = jnp.concatenate([
            gate_grad.astype(jnp.float32).reshape(capacity, blocks, block_units),
            up_grad.astype(jnp.float32).reshape(capacity, blocks, block_units)], axis=2)
        both_weight = jnp.concatenate([
            w_gate.astype(jnp.float32).reshape(features, blocks, block_units),
            w_up.astype(jnp.float32).reshape(features, blocks, block_units)], axis=2)
        pair_grad = block_sum(both_grad, both_weight, "rbf,dbf->rbd").astype(jnp.bfloat16)
        grad_total = grad_total.at[source].add(pair_grad.astype(jnp.float32) * filled[:, None])
        return (out_total, grad_total), (gate_wgrad, up_wgrad, down_grad)

    start_total = jnp.zeros((total_tokens, features), jnp.float32)
    experts_iota = jnp.arange(live_count, dtype=jnp.int32)
    (out_total, grad_total), (gate_grads, up_grads, down_grads) = lax.scan(
        per_expert, (start_total, start_total), (experts_iota, gate_weight, up_weight, down_weight))
    combined = out_total.astype(jnp.bfloat16)
    token_grad = grad_total.astype(jnp.bfloat16)
    return (combined, token_grad, gate_grads, up_grads, down_grads)
```

```python
import functools

import jax
import jax.numpy as jnp
from jax import lax
from jax.experimental import pallas as pl
from jax.experimental.pallas import tpu as pltpu
from jax.sharding import PartitionSpec as P

CAP = 2
PIECES = 4
MESH = pl.DeviceIdType.MESH
F32 = jnp.float32
BF16 = jnp.bfloat16
LAST = (((1,), (1,)), ((), ()))
FIRST = (((0,), (0,)), ((), ()))
STOP = 99


def partner(me, k, n):
    out, bit = 0, 1
    while bit < n:
        digit = lax.rem(me // bit + (k // bit) % 2, 2)
        out = out + digit * bit
        bit *= 2
    return out


def exchange_kernel(
    R,
    E,
    routes,
    gates,
    tok_h,
    grad_h,
    wg_h,
    wu_h,
    wd_h,
    wg_v,
    wu_v,
    wd_v,
    ret,
    place_o,
    w_o,
    tg_v,
    sendb,
    land,
    xf,
    rows,
    hid,
    gg,
    ug,
    part,
    rs,
    back,
    in_sem,
    a2a_s,
    a2a_r,
    ag_s,
    ag_r,
    rs_s,
    rs_r,
    bk_s,
    bk_r,
):
    S = E * CAP
    T, D = tok_h.shape
    U = wg_h.shape[2]
    N = R * S
    CH = D // PIECES
    me_r = lax.axis_index("rep")
    me_e = lax.axis_index("exp")
    peer_r = [partner(me_r, j, R) for j in range(R)]
    peer_e = [partner(me_e, k, E) for k in range(E)]
    loads = [
        pltpu.make_async_copy(tok_h, tg_v.at[0], in_sem.at[0]),
        pltpu.make_async_copy(grad_h, tg_v.at[1], in_sem.at[1]),
        pltpu.make_async_copy(wg_h, wg_v, in_sem.at[2]),
        pltpu.make_async_copy(wu_h, wu_v, in_sem.at[3]),
        pltpu.make_async_copy(wd_h, wd_v, in_sem.at[4]),
    ]
    loads[0].start()
    loads[1].start()
    barrier = pltpu.get_barrier_semaphore()
    for k in range(1, E):
        pl.semaphore_signal(barrier, inc=1, device_id=(me_r, peer_e[k]), device_id_type=MESH)
    for j in range(1, R):
        pl.semaphore_signal(barrier, inc=1, device_id=(peer_r[j], me_e), device_id_type=MESH)

    live = routes[...] < E
    eid = jnp.sum(jnp.where(live, routes[...].astype(F32) + 1.0, 0.0), axis=0, keepdims=True) - 1.0
    w = jnp.sum(jnp.where(live, gates[...], 0.0), axis=0, keepdims=True)
    lanes = lax.broadcasted_iota(jnp.int32, (T, T), 1)
    subs = lax.broadcasted_iota(jnp.int32, (T, T), 0)
    picked = jnp.where(eid == subs[:S].astype(F32), 1.0, 0.0)
    upper = jnp.where(subs < lanes, 1.0, 0.0).astype(BF16)
    before = jnp.dot(picked.astype(BF16), upper, preferred_element_type=F32)
    pos = jnp.sum(picked * before, axis=0, keepdims=True)
    slot = jnp.where(eid >= 0.0, eid * CAP + pos, -1.0)
    placed_t = slot == subs[:S].astype(F32)
    place_t = jnp.where(placed_t, 1.0, 0.0).astype(BF16)
    slot_gate = jnp.sum(jnp.where(placed_t, w, 0.0), axis=1, keepdims=True)

    pl.semaphore_wait(barrier, E + R - 2)

    def forward(t, src, p):
        for j in range(1, R):
            pltpu.make_async_remote_copy(
                src_ref=src,
                dst_ref=land.at[t, me_r, p],
                send_sem=ag_s.at[t],
                recv_sem=ag_r.at[t, j - 1],
                device_id=(peer_r[j], me_e),
                device_id_type=MESH,
            ).start()

    for t in range(2):
        loads[t].wait()
        v = jnp.dot(place_t, tg_v[t], preferred_element_type=F32)
        if t == 1:
            v = slot_gate * v
        for p in range(E):
            sendb[t, p] = v[CAP * p : CAP * p + CAP].astype(BF16)
        if STOP < 1:
            continue
        for k in range(1, E):
            pltpu.make_async_remote_copy(
                src_ref=sendb.at[t, peer_e[k]],
                dst_ref=land.at[t, me_r, me_e],
                send_sem=a2a_s.at[t],
                recv_sem=a2a_r.at[t, k - 1],
                device_id=(me_r, peer_e[k]),
                device_id_type=MESH,
            ).start()
        if STOP >= 2:
            forward(t, sendb.at[t, me_e], me_e)

    for c in loads[2:]:
        c.start()
    place_o[...] = place_t
    w_o[...] = jnp.transpose(jnp.broadcast_to(w, (T, T)))[:, :1]
    for t in range(2):
        land[t, me_r, me_e] = sendb[t, me_e]
        if STOP < 1:
            continue
        for k in range(1, E):
            p = peer_e[k]
            pltpu.make_async_copy(land.at[t, me_r, p], land.at[t, me_r, p], a2a_r.at[t, k - 1]).wait()
            if STOP >= 2:
                forward(t, land.at[t, me_r, p], p)

    def assemble(t):
        for j in range(R):
            r = peer_r[j]
            if j > 0:
                pltpu.make_async_copy(land.at[t, r], land.at[t, r], ag_r.at[t, j - 1]).wait()
            for p in range(E):
                xf[CAP * p : CAP * p + CAP, :] = land[t, r, p].astype(F32)
            rows[t, pl.ds(pl.multiple_of(r * S, S), S), :] = xf[...].astype(BF16)

    def send_part(t, c):
        for j in range(1, R):
            pltpu.make_async_remote_copy(
                src_ref=part.at[t, c, peer_r[j]],
                dst_ref=rs.at[t, c, j - 1],
                send_sem=rs_s.at[t],
                recv_sem=rs_r.at[t, c],
                device_id=(peer_r[j], me_e),
                device_id_type=MESH,
            ).start()

    def give_back(t, c):
        total = part[t, c, me_r].astype(F32)
        pltpu.make_async_copy(rs.at[t, c], rs.at[t, c], rs_r.at[t, c]).wait()
        for j in range(1, R):
            total = total + rs[t, c, j - 1].astype(F32)
        for p in range(E):
            back[t, c, p] = total[CAP * p : CAP * p + CAP].astype(BF16)
        for k in range(1, E):
            pltpu.make_async_remote_copy(
                src_ref=back.at[t, c, peer_e[k]],
                dst_ref=ret.at[t, c, me_e],
                send_sem=bk_s.at[t],
                recv_sem=bk_r.at[t],
                device_id=(me_r, peer_e[k]),
                device_id_type=MESH,
            ).start()
        ret[t, c, me_e] = back[t, c, me_e]

    def weight_grad(out, left, right, c):
        cols = slice(c * CH, c * CH + CH)
        out[0, cols, :] = lax.dot_general(
            left[:, cols], right[...], FIRST, preferred_element_type=F32
        ).astype(BF16)

    x = rows.at[0]
    g = rows.at[1]
    if STOP >= 3:
        assemble(0)
    for c in loads[2:4]:
        c.wait()
    if STOP >= 4:
        gate_pre = jnp.dot(x[...], wg_v[0], preferred_element_type=F32)
        up_pre = jnp.dot(x[...], wu_v[0], preferred_element_type=F32)
        sig = jax.nn.sigmoid(gate_pre)
        active = gate_pre * sig
        hid[...] = (active * up_pre).astype(BF16)
    loads[4].wait()
    for c in range(PIECES if STOP >= 4 else 0):
        cols = slice(c * CH, c * CH + CH)
        o = jnp.dot(hid[...], wd_v[0, :, cols], preferred_element_type=F32)
        part[0, c] = o.astype(BF16).reshape(R, S, CH)
        if STOP >= 7:
            send_part(0, c)

    if STOP >= 3:
        assemble(1)
    if STOP >= 5:
        hg = lax.dot_general(g[...], wd_v[0], LAST, preferred_element_type=F32)
        gg[...] = (hg * up_pre * sig * (1.0 + gate_pre * (1.0 - sig))).astype(BF16)
        ug[...] = (hg * active).astype(BF16)
    for c in range(PIECES if STOP >= 5 else 0):
        cols = slice(c * CH, c * CH + CH)
        o = lax.dot_general(gg[...], wg_v[0, cols, :], LAST, preferred_element_type=F32)
        o = o + lax.dot_general(ug[...], wu_v[0, cols, :], LAST, preferred_element_type=F32)
        part[1, c] = o.astype(BF16).reshape(R, S, CH)
        if STOP >= 7:
            send_part(1, c)

    for c in range(PIECES):
        if STOP >= 7:
            give_back(0, c)
    for c in range(PIECES if STOP >= 6 else 0):
        cols = slice(c * CH, c * CH + CH)
        wd_v[0, :, cols] = lax.dot_general(
            hid[...], g[:, cols], FIRST, preferred_element_type=F32
        ).astype(BF16)
    for c in range(PIECES):
        if STOP >= 6:
            weight_grad(wg_v, x, gg, c)
            weight_grad(wu_v, x, ug, c)
        if STOP >= 7:
            give_back(1, c)

    few, most = pl.ds(0, E - 1), pl.ds(0, R - 1)
    for t in range(2):
        if STOP >= 7:
            pltpu.make_async_copy(ret.at[t, :, few], ret.at[t, :, few], bk_r.at[t]).wait()
    for t in range(2):
        if STOP >= 1:
            pltpu.make_async_copy(sendb.at[t, few], sendb.at[t, few], a2a_s.at[t]).wait()
        if STOP >= 2:
            pltpu.make_async_copy(land.at[t, most], land.at[t, most], ag_s.at[t]).wait()
        if STOP == 2:
            for j in range(1, R):
                pltpu.make_async_copy(land.at[t, 0], land.at[t, 0], ag_r.at[t, j - 1]).wait()
        if STOP >= 7:
            pltpu.make_async_copy(part.at[t, :, most], part.at[t, :, most], rs_s.at[t]).wait()
            pltpu.make_async_copy(back.at[t, :, few], back.at[t, :, few], bk_s.at[t]).wait()


def write_kernel(wg_v, wu_v, wd_v, ret, place, w, comb_o, tgrad_o, wg_o, wu_o, wd_o, res, xf, sem):
    writes = [
        pltpu.make_async_copy(wg_v, wg_o, sem.at[0]),
        pltpu.make_async_copy(wu_v, wu_o, sem.at[1]),
        pltpu.make_async_copy(wd_v, wd_o, sem.at[2]),
        pltpu.make_async_copy(res.at[0], comb_o, sem.at[3]),
        pltpu.make_async_copy(res.at[1], tgrad_o, sem.at[4]),
    ]
    for c in writes[:3]:
        c.start()
    _, pieces, E, _, CH = ret.shape
    for t in range(2):
        for c in range(pieces):
            cols = slice(c * CH, c * CH + CH)
            for p in range(E):
                xf[CAP * p : CAP * p + CAP, :] = ret[t, c, p].astype(F32)
            v = lax.dot_general(place[...], xf[...].astype(BF16), FIRST, preferred_element_type=F32)
            if t == 0:
                v = v * w[...]
            res[t, :, cols] = v.astype(BF16)
        writes[3 + t].start()
    for c in writes:
        c.wait()


def on_device(R, E, tokens, routes, gates, gate_weight, up_weight, down_weight, grad_out):
    T, D = tokens.shape
    U = gate_weight.shape[2]
    S = E * CAP
    N = R * S
    CH = D // PIECES
    vm = pl.BlockSpec(memory_space=pltpu.VMEM)
    hb = pl.BlockSpec(memory_space=pl.ANY)
    dma = pltpu.SemaphoreType.DMA
    sds = jax.ShapeDtypeStruct
    scratch = [
        pltpu.VMEM((2, T, D), BF16),
        pltpu.VMEM((2, E, CAP, D), BF16),
        pltpu.VMEM((2, R, E, CAP, D), BF16),
        pltpu.VMEM((S, D), F32),
        pltpu.VMEM((2, N, D), BF16),
        pltpu.VMEM((N, U), BF16),
        pltpu.VMEM((N, U), BF16),
        pltpu.VMEM((N, U), BF16),
        pltpu.VMEM((2, PIECES, R, S, CH), BF16),
        pltpu.VMEM((2, PIECES, R - 1, S, CH), BF16),
        pltpu.VMEM((2, PIECES, E, CAP, CH), BF16),
    ]
    outs = pl.pallas_call(
        functools.partial(exchange_kernel, R, E),
        out_shape=(
            pltpu.VMEM((1, D, U), BF16),
            pltpu.VMEM((1, D, U), BF16),
            pltpu.VMEM((1, U, D), BF16),
            pltpu.VMEM((2, PIECES, E, CAP, CH), BF16),
            pltpu.VMEM((S, T), BF16),
            pltpu.VMEM((T, 1), F32),
        ),
        in_specs=[vm, vm, hb, hb, hb, hb, hb],
        out_specs=[vm] * 6,
        scratch_shapes=scratch
        + [
            dma((5,)),
            dma((2,)),
            dma((2, E - 1)),
            dma((2,)),
            dma((2, R - 1)),
            dma((2,)),
            dma((2, PIECES)),
            dma((2,)),
            dma((2,)),
        ],
        compiler_params=pltpu.CompilerParams(
            collective_id=0, has_side_effects=True, vmem_limit_bytes=44 * 1024 * 1024
        ),
        name="exchange",
    )(routes.T, gates.T, tokens, grad_out, gate_weight, up_weight, down_weight)
    return pl.pallas_call(
        write_kernel,
        out_shape=(
            sds((T, D), BF16),
            sds((T, D), BF16),
            sds((1, D, U), BF16),
            sds((1, D, U), BF16),
            sds((1, U, D), BF16),
        ),
        in_specs=[vm] * 6,
        out_specs=[hb] * 5,
        scratch_shapes=[
            pltpu.VMEM((2, T, D), BF16),
            pltpu.VMEM((S, CH), F32),
            dma((5,)),
        ],
        compiler_params=pltpu.CompilerParams(vmem_limit_bytes=16 * 1024 * 1024),
        name="write",
    )(*outs)


def solution(mesh):
    placed = (
        P(("rep", "exp"), None),
        P(("rep", "exp"), None),
        P(("rep", "exp"), None),
        P("exp", None, "rep"),
        P("exp", None, "rep"),
        P("exp", "rep", None),
        P(("rep", "exp"), None),
    )
    return jax.shard_map(
        functools.partial(on_device, mesh.shape["rep"], mesh.shape["exp"]),
        mesh=mesh,
        in_specs=placed,
        out_specs=(
            P(("rep", "exp"), None),
            P(("rep", "exp"), None),
            P("exp", None, "rep"),
            P("exp", None, "rep"),
            P("exp", "rep", None),
        ),
        check_vma=False,
    )
```

```python
import functools

import jax
import jax.numpy as jnp
from jax import lax
from jax.experimental import pallas as pl
from jax.experimental.pallas import tpu as pltpu
from jax.sharding import PartitionSpec as P

CAP = 2
PIECES = 4
MESH = pl.DeviceIdType.MESH
F32 = jnp.float32
BF16 = jnp.bfloat16
LAST = (((1,), (1,)), ((), ()))
FIRST = (((0,), (0,)), ((), ()))
RELAYED = 2


def partner(me, k, n):
    out, bit = 0, 1
    while bit < n:
        digit = lax.rem(me // bit + (k // bit) % 2, 2)
        out = out + digit * bit
        bit *= 2
    return out


def axes_of(R):
    inner = 1
    while inner * inner * 4 <= R:
        inner *= 2
    return list(range(1, inner)), list(range(inner, R, inner))


def exchange_kernel(
    R,
    E,
    routes,
    gates,
    tok_h,
    grad_h,
    wg_h,
    wu_h,
    wd_h,
    wg_v,
    wu_v,
    wd_v,
    ret,
    place_o,
    w_o,
    tg_v,
    sendb,
    land,
    xf,
    rows,
    hid,
    gg,
    ug,
    part,
    rs,
    leg,
    back,
    in_sem,
    a2a_s,
    a2a_r,
    ag_s,
    ag_r,
    rs_s,
    rs_r,
    leg_r,
    bk_s,
    bk_r,
):
    S = E * CAP
    T, D = tok_h.shape
    U = wg_h.shape[2]
    N = R * S
    CH = D // PIECES
    axes = axes_of(R)
    me_r = lax.axis_index("rep")
    me_e = lax.axis_index("exp")
    peer_r = [partner(me_r, j, R) for j in range(R)]
    peer_e = [partner(me_e, k, E) for k in range(E)]
    loads = [
        pltpu.make_async_copy(tok_h, tg_v.at[0], in_sem.at[0]),
        pltpu.make_async_copy(grad_h, tg_v.at[1], in_sem.at[1]),
        pltpu.make_async_copy(wg_h, wg_v, in_sem.at[2]),
        pltpu.make_async_copy(wu_h, wu_v, in_sem.at[3]),
        pltpu.make_async_copy(wd_h, wd_v, in_sem.at[4]),
    ]
    loads[0].start()
    loads[1].start()
    barrier = pltpu.get_barrier_semaphore()
    for k in range(1, E):
        pl.semaphore_signal(barrier, inc=1, device_id=(me_r, peer_e[k]), device_id_type=MESH)
    for j in range(1, R):
        pl.semaphore_signal(barrier, inc=1, device_id=(peer_r[j], me_e), device_id_type=MESH)

    live = routes[...] < E
    eid = jnp.sum(jnp.where(live, routes[...].astype(F32) + 1.0, 0.0), axis=0, keepdims=True) - 1.0
    w = jnp.sum(jnp.where(live, gates[...], 0.0), axis=0, keepdims=True)
    lanes = lax.broadcasted_iota(jnp.int32, (T, T), 1)
    subs = lax.broadcasted_iota(jnp.int32, (T, T), 0)
    picked = jnp.where(eid == subs[:S].astype(F32), 1.0, 0.0)
    upper = jnp.where(subs < lanes, 1.0, 0.0).astype(BF16)
    before = jnp.dot(picked.astype(BF16), upper, preferred_element_type=F32)
    pos = jnp.sum(picked * before, axis=0, keepdims=True)
    slot = jnp.where(eid >= 0.0, eid * CAP + pos, -1.0)
    placed_t = slot == subs[:S].astype(F32)
    place_t = jnp.where(placed_t, 1.0, 0.0).astype(BF16)
    slot_gate = jnp.sum(jnp.where(placed_t, w, 0.0), axis=1, keepdims=True)

    pl.semaphore_wait(barrier, E + R - 2)

    def dispatch(t):
        loads[t].wait()
        v = jnp.dot(place_t, tg_v[t], preferred_element_type=F32)
        if t == 1:
            v = slot_gate * v
        for p in range(E):
            sendb[t, p] = v[CAP * p : CAP * p + CAP].astype(BF16)

    def deal(t):
        for k in range(1, E):
            pltpu.make_async_remote_copy(
                src_ref=sendb.at[t, peer_e[k]],
                dst_ref=land.at[t, me_r, me_e],
                send_sem=a2a_s.at[t],
                recv_sem=a2a_r.at[t, k - 1],
                device_id=(me_r, peer_e[k]),
                device_id_type=MESH,
            ).start()

    def forward(t, src, p):
        for j in range(R - 1, 0, -1):
            pltpu.make_async_remote_copy(
                src_ref=src,
                dst_ref=land.at[t, me_r, p],
                send_sem=ag_s.at[t],
                recv_sem=ag_r.at[t, j - 1],
                device_id=(peer_r[j], me_e),
                device_id_type=MESH,
            ).start()

    def pass_on(t, k):
        p = peer_e[k]
        c = land.at[t, me_r, p]
        pltpu.make_async_copy(c, c, a2a_r.at[t, k - 1]).wait()
        forward(t, c, p)

    dispatch(0)
    deal(0)
    forward(0, sendb.at[0, me_e], me_e)
    land[0, me_r, me_e] = sendb[0, me_e]
    dispatch(1)
    place_o[...] = place_t
    w_o[...] = jnp.transpose(jnp.broadcast_to(w, (T, T)))[:, :1]
    forward(1, sendb.at[1, me_e], me_e)
    land[1, me_r, me_e] = sendb[1, me_e]
    deal(1)
    for c in loads[2:]:
        c.start()
    pass_on(0, 1)
    pass_on(1, 1)
    for k in range(2, E):
        pass_on(0, k)
    for k in range(2, E):
        pass_on(1, k)

    def assemble(t):
        for j in range(R):
            r = peer_r[j]
            if j > 0:
                pltpu.make_async_copy(land.at[t, r], land.at[t, r], ag_r.at[t, j - 1]).wait()
            for p in range(E):
                xf[CAP * p : CAP * p + CAP, :] = land[t, r, p].astype(F32)
            rows[t, pl.ds(pl.multiple_of(r * S, S), S), :] = xf[...].astype(BF16)

    def send_block(t, c, src, j, at, sem):
        pltpu.make_async_remote_copy(
            src_ref=src,
            dst_ref=rs.at[t, c, at],
            send_sem=rs_s.at[t],
            recv_sem=sem,
            device_id=(peer_r[j], me_e),
            device_id_type=MESH,
        ).start()

    def relayed(t, c):
        return t == 0 and c < RELAYED

    def relay_plan(c):
        first, second = axes[c % 2], [0] + axes[(c + 1) % 2]
        return first, second, len(first) * len(second)

    def send_part(t, c):
        if relayed(t, c):
            first, second, _ = relay_plan(c)
            for i, f in enumerate(first):
                for q, h in reversed(list(enumerate(second))):
                    send_block(t, c, part.at[t, c, peer_r[f ^ h]], f, i * len(second) + q, rs_r.at[t, c])
        else:
            for j in range(R - 1, 0, -1):
                send_block(t, c, part.at[t, c, peer_r[j]], j, j - 1, rs_r.at[t, c])

    def relay_part(t, c):
        first, second, held = relay_plan(c)
        got = rs.at[t, c, pl.ds(0, held)]
        pltpu.make_async_copy(got, got, rs_r.at[t, c]).wait()
        for q, h in enumerate(second[1:]):
            total = part[t, c, peer_r[h]].astype(F32)
            for i in range(len(first)):
                total = total + rs[t, c, i * len(second) + q + 1].astype(F32)
            leg[c, q] = total.astype(BF16)
            send_block(t, c, leg.at[c, q], h, held + q, leg_r.at[c])

    def give_back(t, c):
        if relayed(t, c):
            first, second, held = relay_plan(c)
            got = rs.at[t, c, pl.ds(held, R - 1 - held)]
            pltpu.make_async_copy(got, got, leg_r.at[c]).wait()
            terms = [i * len(second) for i in range(len(first))] + list(range(held, R - 1))
        else:
            pltpu.make_async_copy(rs.at[t, c], rs.at[t, c], rs_r.at[t, c]).wait()
            terms = range(R - 1)
        total = part[t, c, me_r].astype(F32)
        for i in terms:
            total = total + rs[t, c, i].astype(F32)
        for p in range(E):
            back[t, c, p] = total[CAP * p : CAP * p + CAP].astype(BF16)
        for k in range(E - 1, 0, -1):
            pltpu.make_async_remote_copy(
                src_ref=back.at[t, c, peer_e[k]],
                dst_ref=ret.at[t, c, me_e],
                send_sem=bk_s.at[t],
                recv_sem=bk_r.at[t],
                device_id=(me_r, peer_e[k]),
                device_id_type=MESH,
            ).start()
        ret[t, c, me_e] = back[t, c, me_e]

    pieces = [slice(c * CH, c * CH + CH) for c in range(PIECES)]

    def weight_grad(out, left, right):
        for cols in pieces:
            out[0, cols, :] = lax.dot_general(
                left[:, cols], right[...], FIRST, preferred_element_type=F32
            ).astype(BF16)

    x = rows.at[0]
    g = rows.at[1]
    assemble(0)
    for c in loads[2:4]:
        c.wait()
    gate_pre = jnp.dot(x[...], wg_v[0], preferred_element_type=F32)
    up_pre = jnp.dot(x[...], wu_v[0], preferred_element_type=F32)
    sig = jax.nn.sigmoid(gate_pre)
    active = gate_pre * sig
    hid[...] = (active * up_pre).astype(BF16)
    loads[4].wait()
    for c, cols in enumerate(pieces):
        o = jnp.dot(hid[...], wd_v[0, :, cols], preferred_element_type=F32)
        part[0, c] = o.astype(BF16).reshape(R, S, CH)
        send_part(0, c)

    assemble(1)
    hg = lax.dot_general(g[...], wd_v[0], LAST, preferred_element_type=F32)
    gg[...] = (hg * up_pre * sig * (1.0 + gate_pre * (1.0 - sig))).astype(BF16)
    ug[...] = (hg * active).astype(BF16)
    for c in range(RELAYED):
        relay_part(0, c)
    for c, cols in enumerate(pieces):
        o = lax.dot_general(gg[...], wg_v[0, cols, :], LAST, preferred_element_type=F32)
        o = o + lax.dot_general(ug[...], wu_v[0, cols, :], LAST, preferred_element_type=F32)
        part[1, c] = o.astype(BF16).reshape(R, S, CH)
        send_part(1, c)

    for c in range(PIECES):
        give_back(0, (c + RELAYED) % PIECES)
    for cols in pieces:
        wd_v[0, :, cols] = lax.dot_general(
            hid[...], g[:, cols], FIRST, preferred_element_type=F32
        ).astype(BF16)
    weight_grad(wg_v, x, gg)
    for c in range(PIECES):
        give_back(1, c)
    weight_grad(wu_v, x, ug)

    few, most = pl.ds(0, E - 1), pl.ds(0, R - 1)
    for t in range(2):
        pltpu.make_async_copy(ret.at[t, :, few], ret.at[t, :, few], bk_r.at[t]).wait()
    for t in range(2):
        pltpu.make_async_copy(sendb.at[t, few], sendb.at[t, few], a2a_s.at[t]).wait()
        pltpu.make_async_copy(land.at[t, most], land.at[t, most], ag_s.at[t]).wait()
        pltpu.make_async_copy(part.at[t, :, most], part.at[t, :, most], rs_s.at[t]).wait()
        pltpu.make_async_copy(back.at[t, :, few], back.at[t, :, few], bk_s.at[t]).wait()


def write_kernel(wg_v, wu_v, wd_v, ret, place, w, comb_o, tgrad_o, wg_o, wu_o, wd_o, res, xf, sem):
    writes = [
        pltpu.make_async_copy(wg_v, wg_o, sem.at[0]),
        pltpu.make_async_copy(wu_v, wu_o, sem.at[1]),
        pltpu.make_async_copy(wd_v, wd_o, sem.at[2]),
        pltpu.make_async_copy(res.at[0], comb_o, sem.at[3]),
        pltpu.make_async_copy(res.at[1], tgrad_o, sem.at[4]),
    ]
    for c in writes[:3]:
        c.start()
    _, pieces, E, _, CH = ret.shape
    for t in range(2):
        for c in range(pieces):
            cols = slice(c * CH, c * CH + CH)
            for p in range(E):
                xf[CAP * p : CAP * p + CAP, :] = ret[t, c, p].astype(F32)
            v = lax.dot_general(place[...], xf[...].astype(BF16), FIRST, preferred_element_type=F32)
            if t == 0:
                v = v * w[...]
            res[t, :, cols] = v.astype(BF16)
        writes[3 + t].start()
    for c in writes:
        c.wait()


def on_device(R, E, tokens, routes, gates, gate_weight, up_weight, down_weight, grad_out):
    T, D = tokens.shape
    U = gate_weight.shape[2]
    S = E * CAP
    N = R * S
    CH = D // PIECES
    vm = pl.BlockSpec(memory_space=pltpu.VMEM)
    hb = pl.BlockSpec(memory_space=pl.ANY)
    dma = pltpu.SemaphoreType.DMA
    sds = jax.ShapeDtypeStruct
    scratch = [
        pltpu.VMEM((2, T, D), BF16),
        pltpu.VMEM((2, E, CAP, D), BF16),
        pltpu.VMEM((2, R, E, CAP, D), BF16),
        pltpu.VMEM((S, D), F32),
        pltpu.VMEM((2, N, D), BF16),
        pltpu.VMEM((N, U), BF16),
        pltpu.VMEM((N, U), BF16),
        pltpu.VMEM((N, U), BF16),
        pltpu.VMEM((2, PIECES, R, S, CH), BF16),
        pltpu.VMEM((2, PIECES, R - 1, S, CH), BF16),
        pltpu.VMEM((max(1, RELAYED), len(axes_of(R)[1]), S, CH), BF16),
        pltpu.VMEM((2, PIECES, E, CAP, CH), BF16),
    ]
    outs = pl.pallas_call(
        functools.partial(exchange_kernel, R, E),
        out_shape=(
            pltpu.VMEM((1, D, U), BF16),
            pltpu.VMEM((1, D, U), BF16),
            pltpu.VMEM((1, U, D), BF16),
            pltpu.VMEM((2, PIECES, E, CAP, CH), BF16),
            pltpu.VMEM((S, T), BF16),
            pltpu.VMEM((T, 1), F32),
        ),
        in_specs=[vm, vm, hb, hb, hb, hb, hb],
        out_specs=[vm] * 6,
        scratch_shapes=scratch
        + [
            dma((5,)),
            dma((2,)),
            dma((2, E - 1)),
            dma((2,)),
            dma((2, R - 1)),
            dma((2,)),
            dma((2, PIECES)),
            dma((max(1, RELAYED),)),
            dma((2,)),
            dma((2,)),
        ],
        compiler_params=pltpu.CompilerParams(
            collective_id=0, has_side_effects=True, vmem_limit_bytes=44 * 1024 * 1024
        ),
        name="exchange",
    )(routes.T, gates.T, tokens, grad_out, gate_weight, up_weight, down_weight)
    return pl.pallas_call(
        write_kernel,
        out_shape=(
            sds((T, D), BF16),
            sds((T, D), BF16),
            sds((1, D, U), BF16),
            sds((1, D, U), BF16),
            sds((1, U, D), BF16),
        ),
        in_specs=[vm] * 6,
        out_specs=[hb] * 5,
        scratch_shapes=[
            pltpu.VMEM((2, T, D), BF16),
            pltpu.VMEM((S, CH), F32),
            dma((5,)),
        ],
        compiler_params=pltpu.CompilerParams(vmem_limit_bytes=16 * 1024 * 1024),
        name="write",
    )(*outs)


def solution(mesh):
    placed = (
        P(("rep", "exp"), None),
        P(("rep", "exp"), None),
        P(("rep", "exp"), None),
        P("exp", None, "rep"),
        P("exp", None, "rep"),
        P("exp", "rep", None),
        P(("rep", "exp"), None),
    )
    return jax.shard_map(
        functools.partial(on_device, mesh.shape["rep"], mesh.shape["exp"]),
        mesh=mesh,
        in_specs=placed,
        out_specs=(
            P(("rep", "exp"), None),
            P(("rep", "exp"), None),
            P("exp", None, "rep"),
            P("exp", None, "rep"),
            P("exp", "rep", None),
        ),
        check_vma=False,
    )
```

```python
import functools

import jax
import jax.numpy as jnp
from jax import lax
from jax.experimental import pallas as pl
from jax.experimental.pallas import tpu as pltpu
from jax.sharding import PartitionSpec as P

CAP = 2
PIECES = 7
MESH = pl.DeviceIdType.MESH
F32 = jnp.float32
BF16 = jnp.bfloat16
LAST = (((1,), (1,)), ((), ()))
FIRST = (((0,), (0,)), ((), ()))
RELAYED = 4


def partner(me, k, n):
    out, bit = 0, 1
    while bit < n:
        digit = lax.rem(me // bit + (k // bit) % 2, 2)
        out = out + digit * bit
        bit *= 2
    return out


def axes_of(R):
    inner = 1
    while inner * inner * 4 <= R:
        inner *= 2
    return list(range(1, inner)), list(range(inner, R, inner))


def exchange_kernel(
    R,
    E,
    routes,
    gates,
    tok_h,
    grad_h,
    wg_h,
    wu_h,
    wd_h,
    wg_v,
    wu_v,
    wd_v,
    ret,
    place_o,
    w_o,
    tg_v,
    sendb,
    land,
    xf,
    rows,
    hid,
    gg,
    ug,
    part,
    rs,
    leg,
    back,
    in_sem,
    a2a_s,
    a2a_r,
    ag_s,
    ag_r,
    rs_s,
    rs_r,
    leg_r,
    bk_s,
    bk_r,
):
    S = E * CAP
    T, D = tok_h.shape
    U = wg_h.shape[2]
    N = R * S
    CH = D // PIECES
    axes = axes_of(R)
    me_r = lax.axis_index("rep")
    me_e = lax.axis_index("exp")
    peer_r = [partner(me_r, j, R) for j in range(R)]
    peer_e = [partner(me_e, k, E) for k in range(E)]
    loads = [
        pltpu.make_async_copy(tok_h, tg_v.at[0], in_sem.at[0]),
        pltpu.make_async_copy(grad_h, tg_v.at[1], in_sem.at[1]),
        pltpu.make_async_copy(wg_h, wg_v, in_sem.at[2]),
        pltpu.make_async_copy(wu_h, wu_v, in_sem.at[3]),
        pltpu.make_async_copy(wd_h, wd_v, in_sem.at[4]),
    ]
    barrier = pltpu.get_barrier_semaphore()
    for k in range(1, E):
        pl.semaphore_signal(barrier, inc=1, device_id=(me_r, peer_e[k]), device_id_type=MESH)
    for j in range(1, R):
        pl.semaphore_signal(barrier, inc=1, device_id=(peer_r[j], me_e), device_id_type=MESH)

    loads[0].start()
    loads[1].start()

    live = routes[...] < E
    eid = jnp.sum(jnp.where(live, routes[...].astype(F32) + 1.0, 0.0), axis=0, keepdims=True) - 1.0
    w = jnp.sum(jnp.where(live, gates[...], 0.0), axis=0, keepdims=True)
    lanes = lax.broadcasted_iota(jnp.int32, (T, T), 1)
    subs = lax.broadcasted_iota(jnp.int32, (T, T), 0)
    picked = jnp.where(eid == subs[:S].astype(F32), 1.0, 0.0)
    upper = jnp.where(subs < lanes, 1.0, 0.0).astype(BF16)
    before = jnp.dot(picked.astype(BF16), upper, preferred_element_type=F32)
    pos = jnp.sum(picked * before, axis=0, keepdims=True)
    slot = jnp.where(eid >= 0.0, eid * CAP + pos, -1.0)
    placed_t = slot == subs[:S].astype(F32)
    place_t = jnp.where(placed_t, 1.0, 0.0).astype(BF16)
    slot_gate = jnp.sum(jnp.where(placed_t, w, 0.0), axis=1, keepdims=True)

    pl.semaphore_wait(barrier, E + R - 2)

    def dispatch(t):
        loads[t].wait()
        v = jnp.dot(place_t, tg_v[t], preferred_element_type=F32)
        if t == 1:
            v = slot_gate * v
        for p in range(E):
            sendb[t, p] = v[CAP * p : CAP * p + CAP].astype(BF16)

    def deal(t):
        for k in range(1, E):
            pltpu.make_async_remote_copy(
                src_ref=sendb.at[t, peer_e[k]],
                dst_ref=land.at[t, me_r, me_e],
                send_sem=a2a_s.at[t],
                recv_sem=a2a_r.at[t, k - 1],
                device_id=(me_r, peer_e[k]),
                device_id_type=MESH,
            ).start()

    def forward(t, src, p):
        for j in range(R - 1, 0, -1):
            pltpu.make_async_remote_copy(
                src_ref=src,
                dst_ref=land.at[t, me_r, p],
                send_sem=ag_s.at[t],
                recv_sem=ag_r.at[t, j - 1],
                device_id=(peer_r[j], me_e),
                device_id_type=MESH,
            ).start()

    def pass_on(t, k):
        p = peer_e[k]
        c = land.at[t, me_r, p]
        pltpu.make_async_copy(c, c, a2a_r.at[t, k - 1]).wait()
        forward(t, c, p)

    dispatch(0)
    deal(0)
    forward(0, sendb.at[0, me_e], me_e)
    land[0, me_r, me_e] = sendb[0, me_e]
    dispatch(1)
    place_o[...] = place_t
    w_o[...] = jnp.transpose(jnp.broadcast_to(w, (T, T)))[:, :1]
    forward(1, sendb.at[1, me_e], me_e)
    land[1, me_r, me_e] = sendb[1, me_e]
    deal(1)
    for c in loads[2:]:
        c.start()
    pass_on(0, 1)
    pass_on(1, 1)
    for k in range(2, E):
        pass_on(0, k)
    for k in range(2, E):
        pass_on(1, k)

    def assemble(t):
        for j in range(R):
            r = peer_r[j]
            if j > 0:
                pltpu.make_async_copy(land.at[t, r], land.at[t, r], ag_r.at[t, j - 1]).wait()
            for p in range(E):
                xf[CAP * p : CAP * p + CAP, :] = land[t, r, p].astype(F32)
            rows[t, pl.ds(pl.multiple_of(r * S, S), S), :] = xf[...].astype(BF16)

    def send_block(t, c, src, j, at, sem):
        pltpu.make_async_remote_copy(
            src_ref=src,
            dst_ref=rs.at[t, c, at],
            send_sem=rs_s.at[t],
            recv_sem=sem,
            device_id=(peer_r[j], me_e),
            device_id_type=MESH,
        ).start()

    def relayed(t, c):
        return t == 0 and c < RELAYED

    def relay_plan(c):
        first, second = axes[c % 2], [0] + axes[(c + 1) % 2]
        return first, second, len(first) * len(second)

    def send_part(t, c):
        if relayed(t, c):
            first, second, _ = relay_plan(c)
            for i, f in enumerate(first):
                for q, h in reversed(list(enumerate(second))):
                    send_block(t, c, part.at[t, c, peer_r[f ^ h]], f, i * len(second) + q, rs_r.at[t, c])
        else:
            for j in range(R - 1, 0, -1):
                send_block(t, c, part.at[t, c, peer_r[j]], j, j - 1, rs_r.at[t, c])

    def relay_part(t, c):
        first, second, held = relay_plan(c)
        got = rs.at[t, c, pl.ds(0, held)]
        pltpu.make_async_copy(got, got, rs_r.at[t, c]).wait()
        for q, h in enumerate(second[1:]):
            total = part[t, c, peer_r[h]].astype(F32)
            for i in range(len(first)):
                total = total + rs[t, c, i * len(second) + q + 1].astype(F32)
            leg[c, q] = total.astype(BF16)
            send_block(t, c, leg.at[c, q], h, held + q, leg_r.at[c])

    def give_back(t, c):
        if relayed(t, c):
            first, second, held = relay_plan(c)
            got = rs.at[t, c, pl.ds(held, R - 1 - held)]
            pltpu.make_async_copy(got, got, leg_r.at[c]).wait()
            terms = [i * len(second) for i in range(len(first))] + list(range(held, R - 1))
        else:
            pltpu.make_async_copy(rs.at[t, c], rs.at[t, c], rs_r.at[t, c]).wait()
            terms = range(R - 1)
        total = part[t, c, me_r].astype(F32)
        for i in terms:
            total = total + rs[t, c, i].astype(F32)
        for p in range(E):
            back[t, c, p] = total[CAP * p : CAP * p + CAP].astype(BF16)
        for k in range(E - 1, 0, -1):
            pltpu.make_async_remote_copy(
                src_ref=back.at[t, c, peer_e[k]],
                dst_ref=ret.at[t, c, me_e],
                send_sem=bk_s.at[t],
                recv_sem=bk_r.at[t],
                device_id=(me_r, peer_e[k]),
                device_id_type=MESH,
            ).start()
        ret[t, c, me_e] = back[t, c, me_e]

    pieces = [slice(c * CH, c * CH + CH) for c in range(PIECES)]

    def weight_grad(out, left, right):
        for cols in pieces:
            out[0, cols, :] = lax.dot_general(
                left[:, cols], right[...], FIRST, preferred_element_type=F32
            ).astype(BF16)

    x = rows.at[0]
    g = rows.at[1]
    assemble(0)
    for c in loads[2:4]:
        c.wait()
    gate_pre = jnp.dot(x[...], wg_v[0], preferred_element_type=F32)
    up_pre = jnp.dot(x[...], wu_v[0], preferred_element_type=F32)
    sig = jax.nn.sigmoid(gate_pre)
    active = gate_pre * sig
    hid[...] = (active * up_pre).astype(BF16)
    loads[4].wait()
    for c, cols in enumerate(pieces):
        o = jnp.dot(hid[...], wd_v[0, :, cols], preferred_element_type=F32)
        part[0, c] = o.astype(BF16).reshape(R, S, CH)
        send_part(0, c)

    assemble(1)
    hg = lax.dot_general(g[...], wd_v[0], LAST, preferred_element_type=F32)
    gg[...] = (hg * up_pre * sig * (1.0 + gate_pre * (1.0 - sig))).astype(BF16)
    ug[...] = (hg * active).astype(BF16)
    for c in range(RELAYED):
        relay_part(0, c)
    for c, cols in enumerate(pieces):
        o = lax.dot_general(gg[...], wg_v[0, cols, :], LAST, preferred_element_type=F32)
        o = o + lax.dot_general(ug[...], wu_v[0, cols, :], LAST, preferred_element_type=F32)
        part[1, c] = o.astype(BF16).reshape(R, S, CH)
        send_part(1, c)

    for c in range(PIECES):
        give_back(0, (c + RELAYED) % PIECES)
    for cols in pieces:
        wd_v[0, :, cols] = lax.dot_general(
            hid[...], g[:, cols], FIRST, preferred_element_type=F32
        ).astype(BF16)
    weight_grad(wg_v, x, gg)
    for c in range(PIECES):
        give_back(1, c)
    weight_grad(wu_v, x, ug)

    few, most = pl.ds(0, E - 1), pl.ds(0, R - 1)
    for t in range(2):
        pltpu.make_async_copy(ret.at[t, :, few], ret.at[t, :, few], bk_r.at[t]).wait()
    for t in range(2):
        pltpu.make_async_copy(sendb.at[t, few], sendb.at[t, few], a2a_s.at[t]).wait()
        pltpu.make_async_copy(land.at[t, most], land.at[t, most], ag_s.at[t]).wait()
        pltpu.make_async_copy(part.at[t, :, most], part.at[t, :, most], rs_s.at[t]).wait()
        pltpu.make_async_copy(back.at[t, :, few], back.at[t, :, few], bk_s.at[t]).wait()


def write_kernel(wg_v, wu_v, wd_v, ret, place, w, comb_o, tgrad_o, wg_o, wu_o, wd_o, res, xf, sem):
    writes = [
        pltpu.make_async_copy(wg_v, wg_o, sem.at[0]),
        pltpu.make_async_copy(wu_v, wu_o, sem.at[1]),
        pltpu.make_async_copy(wd_v, wd_o, sem.at[2]),
        pltpu.make_async_copy(res.at[0], comb_o, sem.at[3]),
        pltpu.make_async_copy(res.at[1], tgrad_o, sem.at[4]),
    ]
    for c in writes[:3]:
        c.start()
    _, pieces, E, _, CH = ret.shape
    for t in range(2):
        for c in range(pieces):
            cols = slice(c * CH, c * CH + CH)
            for p in range(E):
                xf[CAP * p : CAP * p + CAP, :] = ret[t, c, p].astype(F32)
            v = lax.dot_general(place[...], xf[...].astype(BF16), FIRST, preferred_element_type=F32)
            if t == 0:
                v = v * w[...]
            res[t, :, cols] = v.astype(BF16)
        writes[3 + t].start()
    for c in writes:
        c.wait()


def on_device(R, E, tokens, routes, gates, gate_weight, up_weight, down_weight, grad_out):
    T, D = tokens.shape
    U = gate_weight.shape[2]
    S = E * CAP
    N = R * S
    CH = D // PIECES
    vm = pl.BlockSpec(memory_space=pltpu.VMEM)
    hb = pl.BlockSpec(memory_space=pl.ANY)
    dma = pltpu.SemaphoreType.DMA
    sds = jax.ShapeDtypeStruct
    scratch = [
        pltpu.VMEM((2, T, D), BF16),
        pltpu.VMEM((2, E, CAP, D), BF16),
        pltpu.VMEM((2, R, E, CAP, D), BF16),
        pltpu.VMEM((S, D), F32),
        pltpu.VMEM((2, N, D), BF16),
        pltpu.VMEM((N, U), BF16),
        pltpu.VMEM((N, U), BF16),
        pltpu.VMEM((N, U), BF16),
        pltpu.VMEM((2, PIECES, R, S, CH), BF16),
        pltpu.VMEM((2, PIECES, R - 1, S, CH), BF16),
        pltpu.VMEM((max(1, RELAYED), len(axes_of(R)[1]), S, CH), BF16),
        pltpu.VMEM((2, PIECES, E, CAP, CH), BF16),
    ]
    outs = pl.pallas_call(
        functools.partial(exchange_kernel, R, E),
        out_shape=(
            pltpu.VMEM((1, D, U), BF16),
            pltpu.VMEM((1, D, U), BF16),
            pltpu.VMEM((1, U, D), BF16),
            pltpu.VMEM((2, PIECES, E, CAP, CH), BF16),
            pltpu.VMEM((S, T), BF16),
            pltpu.VMEM((T, 1), F32),
        ),
        in_specs=[vm, vm, hb, hb, hb, hb, hb],
        out_specs=[vm] * 6,
        scratch_shapes=scratch
        + [
            dma((5,)),
            dma((2,)),
            dma((2, E - 1)),
            dma((2,)),
            dma((2, R - 1)),
            dma((2,)),
            dma((2, PIECES)),
            dma((max(1, RELAYED),)),
            dma((2,)),
            dma((2,)),
        ],
        compiler_params=pltpu.CompilerParams(
            collective_id=0, has_side_effects=True, vmem_limit_bytes=44 * 1024 * 1024
        ),
        name="exchange",
    )(routes.T, gates.T, tokens, grad_out, gate_weight, up_weight, down_weight)
    return pl.pallas_call(
        write_kernel,
        out_shape=(
            sds((T, D), BF16),
            sds((T, D), BF16),
            sds((1, D, U), BF16),
            sds((1, D, U), BF16),
            sds((1, U, D), BF16),
        ),
        in_specs=[vm] * 6,
        out_specs=[hb] * 5,
        scratch_shapes=[
            pltpu.VMEM((2, T, D), BF16),
            pltpu.VMEM((S, CH), F32),
            dma((5,)),
        ],
        compiler_params=pltpu.CompilerParams(vmem_limit_bytes=16 * 1024 * 1024),
        name="write",
    )(*outs)


def solution(mesh):
    placed = (
        P(("rep", "exp"), None),
        P(("rep", "exp"), None),
        P(("rep", "exp"), None),
        P("exp", None, "rep"),
        P("exp", None, "rep"),
        P("exp", "rep", None),
        P(("rep", "exp"), None),
    )
    return jax.shard_map(
        functools.partial(on_device, mesh.shape["rep"], mesh.shape["exp"]),
        mesh=mesh,
        in_specs=placed,
        out_specs=(
            P(("rep", "exp"), None),
            P(("rep", "exp"), None),
            P("exp", None, "rep"),
            P("exp", None, "rep"),
            P("exp", "rep", None),
        ),
        check_vma=False,
    )
```
